32 devices in a mesh: case: 2 (over y), blk: 4 (over z), freq: 4 (over x, core).
Axes of the slice: x: 2, y: 2, z: 4, core: 2. Of those that a mesh axis runs over, the one named last changes fastest.
Arguments:
- geometry: bfloat16 [3, 8192], P(None, ('case', 'blk')), parts along dimension 1, may hold values from -4 to 4
- modes: bfloat16 [4, 8192, 128], P('freq', ('case', 'blk')), parts along dimension 1, may hold values from -6 to 6
- reduced_freq: float32 [16], replicated, may hold values from 0.1 to 1.5
- freq_index: int32 [8, 3], P(('case', 'freq')), parts along dimension 0, may hold values from 0 to 15
Outputs:
- grad_geometry: float32 [3, 8192], P(None, ('case', 'blk', 'freq')), parts along dimension 1
- forces: float32 [8, 2, 32, 32], P(('case', 'freq')), parts along dimension 0
The draws below stay inside these ranges and needn't reach their ends.
There are 2 independent parts, one for each index of `case`. The reference program is written for one: setup_inputs(seed, part) draws one part's arguments, and reference() takes and returns one part's arrays. A program takes and returns all parts, laid end to end along the dimension named above; an argument that names none is the same for every part. Nothing has to cross between parts.
All inputs are finite; a program needn't handle non-finite values.
Results may differ from the reference program's by a relative error of at most 0.003.
Values may be sent and summed in bfloat16 or wider, within the bound.
No kernel may reach another device: no remote copies, remote signals or barrier semaphores. Data moves between devices by JAX's collectives and lax.ppermute only.
A program may use at most 64 MiB of HBM per device.

```python
import math
import jax
import jax.numpy as jnp
from jax import lax

ROWS = 1024
COLS = 32
STEPS = 3
NK = 16
PANELS = 4096
N_BLK = 4
N_FREQ = 4


def with_ends(entries, stream_key, least, largest):
    longest = entries.shape.index(max(entries.shape))
    spots = []
    for shift in (0, 1):
        where = [jax.random.randint(jax.random.fold_in(stream_key, axis), (), 0, length) for axis, length in enumerate(entries.shape)]
        where[longest] = (where[longest] + shift) % entries.shape[longest]
        spots.append(tuple(where))
    return entries.at[spots[0]].set(least).at[spots[1]].set(largest)


def shard_levels(stream_key, shape, pieces, low, high):
    loudness = 1.0
    for axis_at, blocks in pieces:
        draws = jax.random.uniform(jax.random.fold_in(jax.random.fold_in(stream_key, 6), axis_at), (blocks,), jnp.float32, low / len(pieces), high / len(pieces))
        loudness = loudness * jnp.repeat(jnp.exp(draws), shape[axis_at] // blocks).reshape((-1,) + (1,) * (len(shape) - 1 - axis_at))
    return loudness


def noise(key, extent, width, most, cuts=(), kind=jnp.bfloat16):
    values = jax.random.normal(key, extent, jnp.float32) * width
    if len(cuts) > 0:
        values = shard_levels(key, extent, cuts, -0.22, 0.18) * values
    return jnp.clip(values, min=-most, max=most).astype(kind)


def setup_inputs(seed: int = 0, part: int = 0) -> dict:
    streams_of = jax.random.split(jax.random.key(seed), 5)
    own_keys = jax.random.split(jax.random.fold_in(streams_of[4], part), 5)
    geometry = jnp.clip(jax.random.uniform(own_keys[0], (3, PANELS), jnp.float32, -4.0, 4.0) * shard_levels(own_keys[0], (3, PANELS), ((1, 4),), -0.4, 0.0), -4.0, 4.0).astype(jnp.bfloat16)
    modes = noise(own_keys[1], (N_FREQ, PANELS, 4 * COLS), 1.0, 6.0, ((0, 4), (1, 4)))
    reduced_freq = jnp.clip(jnp.exp(jax.random.uniform(streams_of[2], (NK,), jnp.float32, math.log(0.1), math.log(1.5))), 0.1, 1.5)
    freq_index = with_ends(jax.random.randint(own_keys[3], (N_FREQ, STEPS), 0, NK), jax.random.fold_in(own_keys[3], 1), 0, NK - 1).astype(jnp.int32)
    return {"geometry": geometry, "modes": modes, "reduced_freq": reduced_freq, "freq_index": freq_index}


CHORD_SHIFT = 0.5
CORE_SQUARE = 0.25

def pair_terms(recv_geom, recv_modes, send_geom, send_modes, wavenumber):
    columns = recv_modes.shape[1] // 4
    send_count = send_modes.shape[0]
    flipped = jnp.concatenate([send_modes[:, 2 * columns:], send_modes[:, :2 * columns]], axis=1)
    turned = jnp.concatenate([send_modes[:, 3 * columns:], -send_modes[:, 2 * columns:3 * columns], send_modes[:, columns:2 * columns], -send_modes[:, :columns]], axis=1)
    paired = jnp.concatenate([flipped, turned], axis=0)
    coupled = lax.dot_general(recv_modes, paired, (((1,), (1,)), ((), ())), preferred_element_type=jnp.float32, precision=lax.Precision.HIGHEST)
    real_part = coupled[:, :send_count]
    imag_part = coupled[:, send_count:]
    delta_x = recv_geom[0][:, None] + CHORD_SHIFT - send_geom[0][None, :]
    delta_y = recv_geom[1][:, None] - send_geom[1][None, :]
    delta_z = recv_geom[2][:, None] - send_geom[2][None, :]
    inverse = lax.rsqrt(delta_x * delta_x + delta_y * delta_y + delta_z * delta_z + CORE_SQUARE)
    phase = wavenumber * delta_x
    cosine = jnp.cos(phase)
    sine = jnp.sin(phase)
    along = cosine * real_part + sine * imag_part
    across = cosine * imag_part - sine * real_part
    cubed = inverse * inverse * inverse * along
    grad_x = wavenumber * inverse * across - delta_x * cubed
    grad_y = -delta_y * cubed
    grad_z = -delta_z * cubed
    row_grad = jnp.stack([grad_x.sum(axis=1), grad_y.sum(axis=1), grad_z.sum(axis=1)])
    col_grad = -jnp.stack([grad_x.sum(axis=0), grad_y.sum(axis=0), grad_z.sum(axis=0)])
    kernel = jnp.concatenate([cosine * inverse, -sine * inverse], axis=1).astype(jnp.bfloat16)
    kernel = lax.optimization_barrier(kernel).astype(jnp.float32)
    strength = jnp.concatenate([send_modes[:, 2 * columns:], jnp.concatenate([-send_modes[:, 3 * columns:], send_modes[:, 2 * columns:3 * columns]], axis=1)], axis=0)
    pressure = jnp.dot(kernel, strength, preferred_element_type=jnp.float32, precision=lax.Precision.HIGHEST)
    return (row_grad, col_grad, pressure)

def reference(geometry, modes, reduced_freq, freq_index):
    panel_count = geometry.shape[1]
    geom_full = geometry.astype(jnp.float32)
    modes_full = modes.astype(jnp.float32)
    recv_geom = geom_full.reshape(3, N_BLK, ROWS).transpose(1, 0, 2)
    total_grad = jnp.zeros((3, panel_count), jnp.float32)
    table_ids = jnp.arange(NK, dtype=jnp.int32)
    force_list = []
    for group in range(N_FREQ):
        own_modes = modes_full[group]
        recv_modes = own_modes.reshape(N_BLK, ROWS, 4 * COLS)
        pressure_sum = jnp.zeros((N_BLK, ROWS, 2 * COLS), jnp.float32)
        for offset in range(STEPS):
            wavenumber = jnp.sum(jnp.where(table_ids == freq_index[group, offset], reduced_freq, 0.0))
            send_geom = jnp.roll(geom_full, offset * ROWS, axis=1).reshape(3, N_BLK, ROWS).transpose(1, 0, 2)
            send_modes = jnp.roll(own_modes, offset * ROWS, axis=0).reshape(N_BLK, ROWS, 4 * COLS)

            def one_tile(operands, wavenumber=wavenumber):
                return pair_terms(operands[0], operands[1], operands[2], operands[3], wavenumber)
            row_parts, col_parts, pressure = lax.map(one_tile, (recv_geom, recv_modes, send_geom, send_modes))
            row_full = row_parts.transpose(1, 0, 2).reshape(3, panel_count)
            col_full = col_parts.transpose(1, 0, 2).reshape(3, panel_count)
            total_grad = total_grad + row_full + jnp.roll(col_full, -offset * ROWS, axis=1)
            pressure_sum = pressure_sum + pressure
        pressure_flat = pressure_sum.reshape(panel_count, 2 * COLS)
        adj_real = own_modes[:, :COLS]
        adj_imag = own_modes[:, COLS:2 * COLS]
        press_real = pressure_flat[:, :COLS]
        press_imag = pressure_flat[:, COLS:]
        contract = (((0,), (0,)), ((), ()))
        force_real = lax.dot_general(adj_real, press_real, contract, precision=lax.Precision.HIGHEST) + lax.dot_general(adj_imag, press_imag, contract, precision=lax.Precision.HIGHEST)
        force_imag = lax.dot_general(adj_real, press_imag, contract, precision=lax.Precision.HIGHEST) - lax.dot_general(adj_imag, press_real, contract, precision=lax.Precision.HIGHEST)
        force_list.append(jnp.stack([force_real, force_imag]))
    grad_scale = 1.0 / jnp.sqrt(jnp.float32(COLS * STEPS * ROWS * N_FREQ))
    force_scale = 1.0 / jnp.sqrt(jnp.float32(ROWS * panel_count * STEPS))
    return (total_grad * grad_scale, jnp.stack(force_list) * force_scale)
```

```python
import functools
import math

import jax
import jax.numpy as jnp
from jax import lax
from jax.experimental import pallas as pl
from jax.experimental.pallas import tpu as pltpu
from jax.sharding import PartitionSpec as P

CHORD_SHIFT = 0.5
CORE_SQUARE = 0.25
CHUNK = 256

NN = (((1,), (0,)), ((), ()))
NT = (((1,), (1,)), ((), ()))


def passed_along(value, axis, steps):
    count = lax.axis_size(axis)
    pairs = [(source, (source + steps) % count) for source in range(count)]
    return lax.ppermute(value, axis, pairs)


def product(left, right, dims, precision=None):
    return lax.dot_general(
        left, right, dims, preferred_element_type=jnp.float32, precision=precision
    )


def turned_modes(modes, angle):
    flat = modes.astype(jnp.float32).T
    cols = flat.shape[0] // 4
    cosine = jnp.cos(angle)
    sine = jnp.sin(angle)
    real = [flat[:cols], flat[2 * cols : 3 * cols]]
    imag = [flat[cols : 2 * cols], flat[3 * cols :]]
    parts = []
    for re, im in zip(real, imag):
        parts += [re * cosine - im * sine, re * sine + im * cosine]
    return jnp.concatenate(parts, axis=0)


def halves(value):
    high = value.astype(jnp.bfloat16)
    low = (value - high.astype(jnp.float32)).astype(jnp.bfloat16)
    return high, low


def moment_rows(pos):
    count = pos.shape[1]
    return jnp.concatenate(
        [jnp.ones((1, count), jnp.float32), pos, jnp.zeros((12, count), jnp.float32)], axis=0
    ).astype(jnp.bfloat16)


def tile_kernel(
    offset, table_ref, index_ref, rgeom_ref, rmodes_ref, sgeom_ref, smodes_ref,
    row_ref, col_ref, force_ref, sums_ref, moments_ref, back_ref, backm_ref,
):
    count = rmodes_ref.shape[0]
    cols = rmodes_ref.shape[1] // 4
    wave = table_ref[index_ref[0, offset]]
    rpos = rgeom_ref[...].astype(jnp.float32)
    spos = sgeom_ref[...].astype(jnp.float32)
    recv = turned_modes(rmodes_ref[...], wave * (rpos[0:1] + CHORD_SHIFT))
    send = turned_modes(smodes_ref[...], wave * spos[0:1])
    rhigh, rlow = halves(recv)
    shigh, slow = halves(send)
    rboth = jnp.concatenate([rhigh, rlow], axis=0)
    sboth = jnp.concatenate([shigh, slow], axis=0)
    flipped = jnp.concatenate([shigh[2 * cols :], shigh[: 2 * cols]], axis=0)
    paired = jnp.concatenate([flipped, flipped], axis=0)
    rows = jnp.concatenate([rhigh.T, rlow.T], axis=1)
    rmom = moment_rows(rpos)
    smom = moment_rows(spos)
    place = jnp.concatenate([rpos, jnp.zeros((5, count), jnp.float32)], axis=0).T
    for start in range(0, count, CHUNK):
        part = slice(start, start + CHUNK)
        along = product(rows[part], paired, NN)
        dx = (place[part, 0:1] + CHORD_SHIFT) - spos[0:1]
        dy = place[part, 1:2] - spos[1:2]
        dz = place[part, 2:3] - spos[2:3]
        inverse = lax.rsqrt(dx * dx + dy * dy + (dz * dz + CORE_SQUARE))
        kernel = inverse.astype(jnp.bfloat16)
        cubed = ((inverse * inverse) * (inverse * along)).astype(jnp.bfloat16)
        sums_ref[:, part] = product(sboth, kernel, NT)
        moments_ref[:, part] = product(smom, cubed, NT)
        back = product(rboth[:, part], kernel, NN)
        backm = product(rmom[:, part], cubed, NN)
        if start == 0:
            back_ref[...] = back
            backm_ref[...] = backm
        else:
            back_ref[...] += back
            backm_ref[...] += backm
    full = 4 * cols
    ahead = sums_ref[:full] + sums_ref[full:]
    behind = back_ref[:full] + back_ref[full:]

    def quarter(value, k):
        return value[k * cols : (k + 1) * cols]

    def crossed(left, right):
        terms = (
            quarter(left, 0) * quarter(right, 3)
            - quarter(left, 1) * quarter(right, 2)
            + quarter(left, 2) * quarter(right, 1)
            - quarter(left, 3) * quarter(right, 0)
        )
        return jnp.sum(terms, axis=0, keepdims=True)

    row_turn = wave * crossed(recv, ahead)
    col_turn = wave * crossed(behind, send)
    rm = moments_ref[...]
    sm = backm_ref[...]
    row_ref[0:1] = row_turn - ((rpos[0:1] + CHORD_SHIFT) * rm[0:1] - rm[1:2])
    row_ref[1:2] = rm[2:3] - rpos[1:2] * rm[0:1]
    row_ref[2:3] = rm[3:4] - rpos[2:3] * rm[0:1]
    col_ref[0:1] = (sm[1:2] + CHORD_SHIFT * sm[0:1] - spos[0:1] * sm[0:1]) - col_turn
    col_ref[1:2] = sm[2:3] - spos[1:2] * sm[0:1]
    col_ref[2:3] = sm[3:4] - spos[2:3] * sm[0:1]
    gram = product(recv[: 2 * cols], ahead[2 * cols :], NT, lax.Precision.HIGHEST)
    force_ref[0] = gram[:cols, :cols] + gram[cols:, cols:]
    force_ref[1] = gram[:cols, cols:] - gram[cols:, :cols]


def tile_terms(offset, table, index, rgeom, rmodes, sgeom, smodes):
    count, width = rmodes.shape
    cols = width // 4
    smem = pl.BlockSpec(memory_space=pltpu.SMEM)
    vmem = pl.BlockSpec(memory_space=pltpu.VMEM)
    return pl.pallas_call(
        functools.partial(tile_kernel, offset),
        out_shape=(
            jax.ShapeDtypeStruct((3, count), jnp.float32),
            jax.ShapeDtypeStruct((3, count), jnp.float32),
            jax.ShapeDtypeStruct((2, cols, cols), jnp.float32),
        ),
        in_specs=[smem, smem, vmem, vmem, vmem, vmem],
        out_specs=(vmem, vmem, vmem),
        scratch_shapes=[
            pltpu.VMEM((2 * width, count), jnp.float32),
            pltpu.VMEM((16, count), jnp.float32),
            pltpu.VMEM((2 * width, count), jnp.float32),
            pltpu.VMEM((16, count), jnp.float32),
        ],
        compiler_params=pltpu.CompilerParams(vmem_limit_bytes=48 << 20),
        cost_estimate=pl.CostEstimate(
            flops=2 * count * count * width * 6,
            transcendentals=count * count,
            bytes_accessed=4 * count * width,
        ),
    )(table, index, rgeom, rmodes, sgeom, smodes)


def local(geometry, modes, reduced_freq, freq_index):
    row_count = geometry.shape[1]
    own = modes[0]
    columns = own.shape[1] // 4
    steps = freq_index.shape[1]
    freqs = lax.axis_size("freq")
    sending = [(geometry, own)]
    for _ in range(1, steps):
        sending.append(passed_along(sending[-1], "blk", 1))
    total = 0.0
    force = 0.0
    for offset in range(steps):
        row, col, part = tile_terms(
            offset, reduced_freq, freq_index, geometry, own, *sending[offset]
        )
        back = passed_along(col, "blk", -offset) if offset else col
        total = total + row + back
        force = force + part
    grad_scale = 1.0 / math.sqrt(columns * steps * row_count * freqs)
    force_scale = 1.0 / math.sqrt(row_count * row_count * lax.axis_size("blk") * steps)
    share = row_count // freqs
    mine = lax.axis_index("freq")
    pieces = total * grad_scale
    result = lax.psum_scatter(pieces[None], "freq", scatter_dimension=2, tiled=True)[0]
    force_total = lax.psum(force * force_scale, "blk")
    return (result, force_total[None])


def solution(mesh):
    return jax.shard_map(
        local,
        mesh=mesh,
        in_specs=(
            P(None, ("case", "blk")),
            P("freq", ("case", "blk"), None),
            P(),
            P(("case", "freq"), None),
        ),
        out_specs=(P(None, ("case", "blk", "freq")), P(("case", "freq"), None, None, None)),
        check_vma=False,
    )
```

```python
import functools
import math

import jax
import jax.numpy as jnp
from jax import lax
from jax.experimental import pallas as pl
from jax.experimental.pallas import tpu as pltpu
from jax.sharding import PartitionSpec as P

CHORD_SHIFT = 0.5
CORE_SQUARE = 0.25
CHUNK = 256

NN = (((1,), (0,)), ((), ()))
NT = (((1,), (1,)), ((), ()))


def passed_along(value, axis, steps):
    count = lax.axis_size(axis)
    pairs = [(source, (source + steps) % count) for source in range(count)]
    return lax.ppermute(value, axis, pairs)


def product(left, right, dims, precision=None):
    return lax.dot_general(
        left, right, dims, preferred_element_type=jnp.float32, precision=precision
    )


def turned_modes(modes, angle):
    flat = modes.astype(jnp.float32).T
    cols = flat.shape[0] // 4
    cosine = jnp.cos(angle)
    sine = jnp.sin(angle)
    real = [flat[:cols], flat[2 * cols : 3 * cols]]
    imag = [flat[cols : 2 * cols], flat[3 * cols :]]
    parts = []
    for re, im in zip(real, imag):
        parts += [re * cosine - im * sine, re * sine + im * cosine]
    return jnp.concatenate(parts, axis=0)


def halves(value):
    high = value.astype(jnp.bfloat16)
    low = (value - high.astype(jnp.float32)).astype(jnp.bfloat16)
    return high, low


def moment_rows(pos):
    count = pos.shape[1]
    return jnp.concatenate(
        [jnp.ones((1, count), jnp.float32), pos, jnp.zeros((12, count), jnp.float32)], axis=0
    ).astype(jnp.bfloat16)


def tile_kernel(
    offset, plan, table_ref, index_ref, rgeom_ref, rmodes_ref, sgeom_ref, smodes_ref, *refs
):
    held = refs[: plan.held]
    grads = refs[plan.held : plan.held + plan.grads]
    force_ref, sums_ref, moments_ref, back_ref, backm_ref = refs[plan.held + plan.grads :]
    count = rmodes_ref.shape[0]
    cols = rmodes_ref.shape[1] // 4
    wave = table_ref[index_ref[0, offset]]
    rpos = rgeom_ref[...].astype(jnp.float32)
    spos = sgeom_ref[...].astype(jnp.float32)
    recv = turned_modes(rmodes_ref[...], wave * (rpos[0:1] + CHORD_SHIFT))
    send = turned_modes(smodes_ref[...], wave * spos[0:1])
    rhigh, rlow = halves(recv)
    shigh, slow = halves(send)
    rboth = jnp.concatenate([rhigh, rlow], axis=0)
    sboth = jnp.concatenate([shigh, slow], axis=0)
    flipped = jnp.concatenate([shigh[2 * cols :], shigh[: 2 * cols]], axis=0)
    paired = jnp.concatenate([flipped, flipped], axis=0)
    rows = jnp.concatenate([rhigh.T, rlow.T], axis=1)
    rmom = moment_rows(rpos)
    smom = moment_rows(spos)
    place = jnp.concatenate([rpos, jnp.zeros((5, count), jnp.float32)], axis=0).T
    for start in range(0, count, CHUNK):
        part = slice(start, start + CHUNK)
        along = product(rows[part], paired, NN)
        dx = (place[part, 0:1] + CHORD_SHIFT) - spos[0:1]
        dy = place[part, 1:2] - spos[1:2]
        dz = place[part, 2:3] - spos[2:3]
        inverse = lax.rsqrt(dx * dx + dy * dy + (dz * dz + CORE_SQUARE))
        kernel = inverse.astype(jnp.bfloat16)
        cubed = ((inverse * inverse) * (inverse * along)).astype(jnp.bfloat16)
        sums_ref[:, part] = product(sboth, kernel, NT)
        moments_ref[:, part] = product(smom, cubed, NT)
        back = product(rboth[:, part], kernel, NN)
        backm = product(rmom[:, part], cubed, NN)
        if start == 0:
            back_ref[...] = back
            backm_ref[...] = backm
        else:
            back_ref[...] += back
            backm_ref[...] += backm
    full = 4 * cols
    ahead = sums_ref[:full] + sums_ref[full:]
    behind = back_ref[:full] + back_ref[full:]

    def quarter(value, k):
        return value[k * cols : (k + 1) * cols]

    def crossed(left, right):
        terms = (
            quarter(left, 0) * quarter(right, 3)
            - quarter(left, 1) * quarter(right, 2)
            + quarter(left, 2) * quarter(right, 1)
            - quarter(left, 3) * quarter(right, 0)
        )
        return jnp.sum(terms, axis=0, keepdims=True)

    row_turn = wave * crossed(recv, ahead)
    col_turn = wave * crossed(behind, send)
    rm = moments_ref[...]
    sm = backm_ref[...]
    row = jnp.concatenate(
        [
            row_turn - ((rpos[0:1] + CHORD_SHIFT) * rm[0:1] - rm[1:2]),
            rm[2:3] - rpos[1:2] * rm[0:1],
            rm[3:4] - rpos[2:3] * rm[0:1],
        ],
        axis=0,
    )
    col = jnp.concatenate(
        [
            (sm[1:2] + CHORD_SHIFT * sm[0:1] - spos[0:1] * sm[0:1]) - col_turn,
            sm[2:3] - spos[1:2] * sm[0:1],
            sm[3:4] - spos[2:3] * sm[0:1],
        ],
        axis=0,
    )
    gram = product(recv[: 2 * cols], ahead[2 * cols :], NT, lax.Precision.HIGHEST)
    force_real = (gram[:cols, :cols] + gram[cols:, cols:]) * plan.force_scale
    force_imag = (gram[:cols, cols:] - gram[cols:, :cols]) * plan.force_scale
    row = row * plan.grad_scale
    col = col * plan.grad_scale
    if plan.role == "own":
        grads[0][...] = row + col
        force_ref[0] = force_real
        force_ref[1] = force_imag
    elif plan.role == "below":
        grads[0][...] = held[0][...] + row
        grads[1][...] = col
        force_ref[0] = held[1][0] + force_real
        force_ref[1] = held[1][1] + force_imag
    else:
        grads[0][...] = row
        grads[1][...] = held[0][...] + col
        force_ref[0] = held[1][0] + force_real
        force_ref[1] = held[1][1] + force_imag


class Plan:
    def __init__(self, role, grad_scale, force_scale):
        self.role = role
        self.grad_scale = grad_scale
        self.force_scale = force_scale
        self.held = 0 if role == "own" else 2
        self.grads = 1 if role == "own" else 2


def tile_terms(offset, plan, table, index, recv, send, *held):
    count, width = recv[1].shape
    cols = width // 4
    smem = pl.BlockSpec(memory_space=pltpu.SMEM)
    vmem = pl.BlockSpec(memory_space=pltpu.VMEM)
    grad = jax.ShapeDtypeStruct((3, count), jnp.float32)
    force = jax.ShapeDtypeStruct((2, cols, cols), jnp.float32)
    return pl.pallas_call(
        functools.partial(tile_kernel, offset, plan),
        out_shape=(grad,) * plan.grads + (force,),
        in_specs=[smem, smem] + [vmem] * (4 + plan.held),
        out_specs=(vmem,) * (plan.grads + 1),
        scratch_shapes=[
            pltpu.VMEM((2 * width, count), jnp.float32),
            pltpu.VMEM((16, count), jnp.float32),
            pltpu.VMEM((2 * width, count), jnp.float32),
            pltpu.VMEM((16, count), jnp.float32),
        ],
        name="tile_" + plan.role,
        compiler_params=pltpu.CompilerParams(vmem_limit_bytes=48 << 20),
        cost_estimate=pl.CostEstimate(
            flops=2 * count * count * width * 6,
            transcendentals=count * count,
            bytes_accessed=4 * count * width,
        ),
    )(table, index, *recv, *send, *held)


def local(geometry, modes, reduced_freq, freq_index):
    row_count = geometry.shape[1]
    own = (geometry, modes[0])
    columns = modes.shape[2] // 4
    steps = freq_index.shape[1]
    blocks = lax.axis_size("blk")
    freqs = lax.axis_size("freq")
    grad_scale = 1.0 / math.sqrt(columns * steps * row_count * freqs)
    force_scale = 1.0 / math.sqrt(row_count * row_count * blocks * steps)
    below = passed_along(own, "blk", 1)
    above = passed_along(own, "blk", -1)
    def terms(offset, role, *operands):
        plan = Plan(role, grad_scale, force_scale)
        return tile_terms(offset, plan, reduced_freq, freq_index, *operands)

    mine, force = terms(0, "own", own, own)
    mine, down, force = terms(1, "below", own, below, mine, force)
    up, down, force = terms(2, "across", above, below, down, force)
    total = mine + passed_along(down, "blk", -1) + passed_along(up, "blk", 1)
    if blocks == 4:
        force_total = force
        for shift in (-1, 1, 2):
            force_total = force_total + passed_along(force, "blk", shift)
    else:
        force_total = lax.psum(force, "blk")
    share = row_count // freqs
    place = lax.axis_index("freq")
    result = None
    for flip in range(freqs):
        piece = lax.dynamic_slice_in_dim(total, (place ^ flip) * share, share, axis=1)
        if flip:
            pairs = [(source, source ^ flip) for source in range(freqs)]
            result = result + lax.ppermute(piece, "freq", pairs)
        else:
            result = piece
    return (result, force_total[None])


def solution(mesh):
    return jax.shard_map(
        local,
        mesh=mesh,
        in_specs=(
            P(None, ("case", "blk")),
            P("freq", ("case", "blk"), None),
            P(),
            P(("case", "freq"), None),
        ),
        out_specs=(P(None, ("case", "blk", "freq")), P(("case", "freq"), None, None, None)),
        check_vma=False,
    )
```

```python
import functools
import math

import jax
import jax.numpy as jnp
from jax import lax
from jax.experimental import pallas as pl
from jax.experimental.pallas import tpu as pltpu
from jax.sharding import PartitionSpec as P

CHORD_SHIFT = 0.5
CORE_SQUARE = 0.25
CHUNK = 512

NN = (((1,), (0,)), ((), ()))
NT = (((1,), (1,)), ((), ()))


def passed_along(value, axis, steps):
    count = lax.axis_size(axis)
    pairs = [(source, (source + steps) % count) for source in range(count)]
    return lax.ppermute(value, axis, pairs)


def exchanged(value, axis, flip):
    pairs = [(source, source ^ flip) for source in range(lax.axis_size(axis))]
    return lax.ppermute(value, axis, pairs)


def product(left, right, dims, precision=None):
    return lax.dot_general(
        left, right, dims, preferred_element_type=jnp.float32, precision=precision
    )


def cosine_of(angle):
    turns = jnp.floor(angle * (0.5 / math.pi) + 0.5)
    half = 0.5 * ((angle - turns * 6.28125) - turns * (2.0 * math.pi - 6.28125))
    square = half * half
    value = 1.0 / math.factorial(12)
    for order in (10, 8, 6, 4, 2, 0):
        sign = -1.0 if order % 4 == 2 else 1.0
        value = value * square + sign / math.factorial(order)
    return 2.0 * value * value - 1.0


def turned_modes(flat, cosine, sine):
    cols = flat.shape[0] // 4
    real = [flat[:cols], flat[2 * cols : 3 * cols]]
    imag = [flat[cols : 2 * cols], flat[3 * cols :]]
    parts = []
    for re, im in zip(real, imag):
        parts += [re * cosine - im * sine, re * sine + im * cosine]
    return jnp.concatenate(parts, axis=0)


def crosswise(value):
    cols = value.shape[0] // 4
    p, q, r, s = (value[k * cols : (k + 1) * cols] for k in range(4))
    return jnp.concatenate([-s, r, -q, p], axis=0)


def halves(value):
    high = value.astype(jnp.bfloat16)
    low = (value - high.astype(jnp.float32)).astype(jnp.bfloat16)
    return high, low


def moment_rows(pos):
    count = pos.shape[1]
    return jnp.concatenate(
        [jnp.ones((1, count), jnp.float32), pos, jnp.zeros((12, count), jnp.float32)], axis=0
    ).astype(jnp.bfloat16)


def tile_kernel(
    offset, plan, table_ref, index_ref, rgeom_ref, rmodes_ref, sgeom_ref, smodes_ref, *refs
):
    held = refs[: plan.held]
    grads = refs[plan.held : plan.held + plan.grads]
    force_ref, back_ref, backm_ref, row_ref, *rest = refs[plan.held + plan.grads :]
    if plan.role == "own":
        geom_buf, modes_buf, sems = rest
        copies = [
            pltpu.make_async_copy(rgeom_ref, geom_buf, sems.at[0]),
            pltpu.make_async_copy(rmodes_ref, modes_buf, sems.at[1]),
        ]
        for copy in copies:
            copy.start()
        for copy in copies:
            copy.wait()
        rgeom_ref, rmodes_ref = geom_buf, modes_buf
    count, full = rmodes_ref.shape
    cols = full // 4
    wave = table_ref[index_ref[0, offset]]
    rpos = rgeom_ref[...].astype(jnp.float32)
    rflat = rmodes_ref[...].astype(jnp.float32).T
    if plan.role == "own":
        spos, sflat = rpos, rflat
    else:
        spos = sgeom_ref[...].astype(jnp.float32)
        sflat = smodes_ref[...].astype(jnp.float32).T
    rangle = wave * (rpos[0:1] + CHORD_SHIFT)
    sangle = wave * spos[0:1]
    quarter_turn = 0.5 * math.pi
    circle = cosine_of(
        jnp.concatenate([rangle, rangle - quarter_turn, sangle, sangle - quarter_turn], axis=0)
    )
    recv = turned_modes(rflat, circle[0:1], circle[1:2])
    send = turned_modes(sflat, circle[2:3], circle[3:4])
    rhigh, rlow = halves(recv)
    shigh, slow = halves(send)
    rboth = jnp.concatenate([rhigh, rlow[: 2 * cols]], axis=0)
    rows = jnp.concatenate([crosswise(rhigh), crosswise(rlow)], axis=0).T
    cross = crosswise(jnp.concatenate([shigh[2 * cols :], shigh[: 2 * cols]], axis=0))
    paired = jnp.concatenate([cross, cross], axis=0)
    srows = jnp.concatenate([shigh, slow[2 * cols :], slow[2 * cols :]], axis=0).T
    rmom = moment_rows(rpos)
    smom = moment_rows(spos)
    smom_rows = jnp.concatenate(
        [smom.astype(jnp.float32), jnp.zeros((full - 16, count), jnp.float32)], axis=0
    ).T.astype(jnp.bfloat16)
    place = jnp.concatenate([rpos, jnp.zeros((5, count), jnp.float32)], axis=0).T
    lane = lax.broadcasted_iota(jnp.int32, (CHUNK, full), 1)
    def stage_l(start):
        return product(rows[start:start+CHUNK], paired, NN)

    def stage_v(start, along):
        part = slice(start, start + CHUNK)
        dx = (place[part, 0:1] + CHORD_SHIFT) - spos[0:1]
        dy = place[part, 1:2] - spos[1:2]
        dz = place[part, 2:3] - spos[2:3]
        inverse = lax.rsqrt(dx * dx + dy * dy + (dz * dz + CORE_SQUARE))
        kernel = inverse.astype(jnp.bfloat16)
        cubed = ((inverse * inverse) * (inverse * along)).astype(jnp.bfloat16)
        return kernel, cubed

    def stage_m(start, kernel, cubed):
        part = slice(start, start + CHUNK)
        ahead = product(kernel, srows[:, :full], NN)
        moments = product(cubed, smom_rows, NN)
        back = product(rboth[:, part], kernel, NN)
        backm = product(rmom[:, part], cubed, NN)
        both = rows[part].astype(jnp.float32)
        turn = jnp.sum((both[:, :full] + both[:, full:]) * ahead, axis=1, keepdims=True)
        row_ref[:, part] = jnp.where(lane == 4, turn, moments).T[:8]
        return back, backm

    starts = list(range(0, count, CHUNK))
    along = stage_l(0)
    pair = stage_v(0, along)
    for k, start in enumerate(starts):
        nxt = None
        if k + 1 < len(starts):
            along = stage_l(starts[k + 1])
        back, backm = stage_m(start, *pair)
        if k + 1 < len(starts):
            pair = stage_v(starts[k + 1], along)
        if k == 0:
            back_ref[...] = back
            backm_ref[...] = backm
        else:
            back_ref[...] += back
            backm_ref[...] += backm
    behind = back_ref[: full] + jnp.concatenate(
        [back_ref[full:], jnp.zeros((2 * cols, count), jnp.float32)], axis=0
    )

    def quarter(value, k):
        return value[k * cols : (k + 1) * cols]

    col_turn = wave * jnp.sum(
        quarter(behind, 0) * quarter(send, 3)
        - quarter(behind, 1) * quarter(send, 2)
        + quarter(behind, 2) * quarter(send, 1)
        - quarter(behind, 3) * quarter(send, 0),
        axis=0,
        keepdims=True,
    )
    rm = row_ref[...]
    sm = backm_ref[...]
    row = jnp.concatenate(
        [
            wave * rm[4:5] - ((rpos[0:1] + CHORD_SHIFT) * rm[0:1] - rm[1:2]),
            rm[2:3] - rpos[1:2] * rm[0:1],
            rm[3:4] - rpos[2:3] * rm[0:1],
        ],
        axis=0,
    ) * plan.grad_scale
    col = jnp.concatenate(
        [
            (sm[1:2] + CHORD_SHIFT * sm[0:1] - spos[0:1] * sm[0:1]) - col_turn,
            sm[2:3] - spos[1:2] * sm[0:1],
            sm[3:4] - spos[2:3] * sm[0:1],
        ],
        axis=0,
    ) * plan.grad_scale
    bhigh, blow = halves(behind[: 2 * cols])
    gram = product(jnp.concatenate([bhigh, blow], axis=0), srows, NN)
    gram = (
        gram[: 2 * cols, 2 * cols : full]
        + gram[2 * cols :, 2 * cols : full]
        + gram[: 2 * cols, full : full + 2 * cols]
    )
    force_real = (gram[:cols, :cols] + gram[cols:, cols:]) * plan.force_scale
    force_imag = (gram[:cols, cols:] - gram[cols:, :cols]) * plan.force_scale
    if plan.role == "own":
        grads[0][...] = row + col
        force_ref[0] = force_real
        force_ref[1] = force_imag
    else:
        grads[0][...] = held[0][...] + row
        grads[1][...] = col
        force_ref[0] = held[1][0] + force_real
        force_ref[1] = held[1][1] + force_imag


class Plan:
    def __init__(self, role, grad_scale, force_scale):
        self.role = role
        self.grad_scale = grad_scale
        self.force_scale = force_scale
        self.held = 0 if role == "own" else 2
        self.grads = 1 if role == "own" else 2


def tile_terms(offset, plan, table, index, recv, send, *held):
    count, width = recv[1].shape
    cols = width // 4
    smem = pl.BlockSpec(memory_space=pltpu.SMEM)
    vmem = pl.BlockSpec(memory_space=pltpu.VMEM)
    grad = jax.ShapeDtypeStruct((3, count), jnp.float32)
    force = jax.ShapeDtypeStruct((2, cols, cols), jnp.float32)
    operands = [vmem] * 4
    extra = []
    if plan.role == "own":
        operands = [pl.BlockSpec(memory_space=pl.ANY)] * 4
        extra = [
            pltpu.VMEM(recv[0].shape, recv[0].dtype),
            pltpu.VMEM(recv[1].shape, recv[1].dtype),
            pltpu.SemaphoreType.DMA((2,)),
        ]
    return pl.pallas_call(
        functools.partial(tile_kernel, offset, plan),
        out_shape=(grad,) * plan.grads + (force,),
        in_specs=[smem, smem] + operands + [vmem] * plan.held,
        out_specs=(vmem,) * (plan.grads + 1),
        scratch_shapes=[
            pltpu.VMEM((width + 2 * cols, count), jnp.float32),
            pltpu.VMEM((16, count), jnp.float32),
            pltpu.VMEM((8, count), jnp.float32),
        ]
        + extra,
        name="tile_%d" % offset,
        compiler_params=pltpu.CompilerParams(vmem_limit_bytes=48 << 20),
        cost_estimate=pl.CostEstimate(
            flops=2 * count * count * width * 6,
            transcendentals=count * count,
            bytes_accessed=4 * count * width,
        ),
    )(table, index, *recv, *send, *held)


def local(geometry, modes, reduced_freq, freq_index):
    row_count = geometry.shape[1]
    own = (geometry, modes[0])
    columns = modes.shape[2] // 4
    steps = freq_index.shape[1]
    blocks = lax.axis_size("blk")
    freqs = lax.axis_size("freq")
    grad_scale = 1.0 / math.sqrt(columns * steps * row_count * freqs)
    force_scale = 1.0 / math.sqrt(row_count * row_count * blocks * steps)

    def terms(offset, *operands):
        plan = Plan("sent" if offset else "own", grad_scale, force_scale)
        return tile_terms(offset, plan, reduced_freq, freq_index, *operands)

    sender = passed_along(own, "blk", 1)
    mine, force = terms(0, own, own)
    sender, mine = lax.optimization_barrier((sender, mine))
    returned = []
    for offset in range(1, steps):
        current = sender
        if offset + 1 < steps:
            sender = passed_along(current, "blk", 1)
        mine, back, force = terms(offset, own, current, mine, force)
        returned.append(passed_along(back, "blk", -offset))
    total = mine
    for back in returned:
        total = total + back
    if blocks == 4:
        pair = force + passed_along(force, "blk", -2)
        force_total = pair + exchanged(pair, "blk", 1)
    else:
        force_total = lax.psum(force, "blk")
    share = row_count // freqs
    place = lax.axis_index("freq")
    result = lax.dynamic_slice_in_dim(total, place * share, share, axis=1)
    for flip in range(1, freqs):
        piece = lax.dynamic_slice_in_dim(total, (place ^ flip) * share, share, axis=1)
        result = result + exchanged(piece, "freq", flip)
    return (result, force_total[None])


def solution(mesh):
    return jax.shard_map(
        local,
        mesh=mesh,
        in_specs=(
            P(None, ("case", "blk")),
            P("freq", ("case", "blk"), None),
            P(),
            P(("case", "freq"), None),
        ),
        out_specs=(P(None, ("case", "blk", "freq")), P(("case", "freq"), None, None, None)),
        check_vma=False,
    )
```

```python
import functools
import math

import jax
import jax.numpy as jnp
from jax import lax
from jax.experimental import pallas as pl
from jax.experimental.pallas import tpu as pltpu
from jax.sharding import PartitionSpec as P

CHORD_SHIFT = 0.5
CORE_SQUARE = 0.25
CHUNK = 512

NN = (((1,), (0,)), ((), ()))
NT = (((1,), (1,)), ((), ()))


def passed_along(value, axis, steps):
    count = lax.axis_size(axis)
    pairs = [(source, (source + steps) % count) for source in range(count)]
    return lax.ppermute(value, axis, pairs)


def exchanged(value, axis, flip):
    pairs = [(source, source ^ flip) for source in range(lax.axis_size(axis))]
    return lax.ppermute(value, axis, pairs)


def product(left, right, dims, precision=None):
    return lax.dot_general(
        left, right, dims, preferred_element_type=jnp.float32, precision=precision
    )


def cosine_of(angle):
    turns = jnp.floor(angle * (0.5 / math.pi) + 0.5)
    half = 0.5 * ((angle - turns * 6.28125) - turns * (2.0 * math.pi - 6.28125))
    square = half * half
    value = 1.0 / math.factorial(12)
    for order in (10, 8, 6, 4, 2, 0):
        sign = -1.0 if order % 4 == 2 else 1.0
        value = value * square + sign / math.factorial(order)
    return 2.0 * value * value - 1.0


def turned_modes(flat, cosine, sine):
    cols = flat.shape[0] // 4
    real = [flat[:cols], flat[2 * cols : 3 * cols]]
    imag = [flat[cols : 2 * cols], flat[3 * cols :]]
    parts = []
    for re, im in zip(real, imag):
        parts += [re * cosine - im * sine, re * sine + im * cosine]
    return jnp.concatenate(parts, axis=0)


def crosswise(value):
    cols = value.shape[0] // 4
    p, q, r, s = (value[k * cols : (k + 1) * cols] for k in range(4))
    return jnp.concatenate([-s, r, -q, p], axis=0)


def halves(value):
    high = value.astype(jnp.bfloat16)
    low = (value - high.astype(jnp.float32)).astype(jnp.bfloat16)
    return high, low


def moment_rows(pos):
    count = pos.shape[1]
    return jnp.concatenate(
        [jnp.ones((1, count), jnp.float32), pos, jnp.zeros((12, count), jnp.float32)], axis=0
    ).astype(jnp.bfloat16)


def tile_kernel(offset, plan, *refs):
    refs = list(refs)

    def taken(number):
        return [refs.pop(0) for _ in range(number)]

    if plan.role == "own":
        table_ref, index_ref, rgeom_ref, rmodes_ref = taken(4)
    else:
        waves_ref, rgeom_ref, rmodes_ref, sgeom_ref, smodes_ref = taken(5)
    if plan.emits:
        (next_ref,) = taken(1)
    if plan.ready:
        near_ref, cube_ref, rows_ref, rboth_ref = taken(4)
    held = taken(plan.held)
    grads = taken(plan.grads)
    if not plan.last:
        (force_ref,) = taken(1)
    if plan.role == "own":
        waves_out, geom_out, modes_out = taken(3)
    if plan.emits:
        near_out, cube_out, rows_out, rboth_out = taken(4)
    back_ref, backm_ref, row_ref = taken(3)
    if plan.role == "own":
        table_buf, index_buf, sems = taken(3)
        copies = [
            pltpu.make_async_copy(rgeom_ref, geom_out, sems.at[0]),
            pltpu.make_async_copy(rmodes_ref, modes_out, sems.at[1]),
            pltpu.make_async_copy(table_ref, table_buf, sems.at[2]),
            pltpu.make_async_copy(index_ref, index_buf, sems.at[3]),
        ]
        for copy in copies:
            copy.start()
        for copy in copies:
            copy.wait()
        rgeom_ref, rmodes_ref = geom_out, modes_out
        wave = table_buf[index_buf[0, offset]]
        for step in range(index_buf.shape[1]):
            value = table_buf[index_buf[0, step]]
            waves_out[step : step + 1] = jnp.full((1, waves_out.shape[1]), value, jnp.float32)
    else:
        wave = waves_ref[offset : offset + 1, 0:1]
    count, full = rmodes_ref.shape
    cols = full // 4
    starts = list(range(0, count, CHUNK))
    rpos = rgeom_ref[...].astype(jnp.float32)
    place = jnp.concatenate([rpos, jnp.zeros((5, count), jnp.float32)], axis=0).T
    if plan.ready:
        back_ref[...] = product(rboth_ref[...], near_ref[...], NN)
    else:
        rflat = rmodes_ref[...].astype(jnp.float32).T
    if plan.role == "own":
        spos, sflat = rpos, rflat
    else:
        spos = sgeom_ref[...].astype(jnp.float32)
        sflat = smodes_ref[...].astype(jnp.float32).T
    angles = [wave * spos[0:1]]
    if not plan.ready:
        angles.append(wave * (rpos[0:1] + CHORD_SHIFT))
    if plan.emits:
        angles.append(waves_ref[offset + 1 : offset + 2, 0:1] * (rpos[0:1] + CHORD_SHIFT))
    quarter_turn = 0.5 * math.pi
    circle = cosine_of(
        jnp.concatenate(angles + [angle - quarter_turn for angle in angles], axis=0)
    )
    turns = [(circle[k : k + 1], circle[len(angles) + k :][:1]) for k in range(len(angles))]

    def receiving(turn):
        high, low = halves(turned_modes(rflat, *turn))
        both = jnp.concatenate([high, low[: 2 * cols]], axis=0)
        return both, jnp.concatenate([crosswise(high), crosswise(low)], axis=0).T

    def reciprocal(start, points):
        part = slice(start, start + CHUNK)
        dx = (place[part, 0:1] + CHORD_SHIFT) - points[0:1]
        dy = place[part, 1:2] - points[1:2]
        dz = place[part, 2:3] - points[2:3]
        return lax.rsqrt(dx * dx + dy * dy + (dz * dz + CORE_SQUARE))

    send = turned_modes(sflat, *turns[0])
    shigh, slow = halves(send)
    if plan.ready:
        rows = rows_ref[...]
    else:
        rboth, rows = receiving(turns[1])
    cross = crosswise(jnp.concatenate([shigh[2 * cols :], shigh[: 2 * cols]], axis=0))
    paired = jnp.concatenate([cross, cross], axis=0)
    srows = jnp.concatenate([shigh, slow[2 * cols :], slow[2 * cols :]], axis=0).T
    rmom = moment_rows(rpos)
    smom = moment_rows(spos)
    smom_rows = jnp.concatenate(
        [smom.astype(jnp.float32), jnp.zeros((full - 16, count), jnp.float32)], axis=0
    ).T.astype(jnp.bfloat16)
    lane = lax.broadcasted_iota(jnp.int32, (CHUNK, full), 1)

    def stage_l(start):
        return product(rows[start : start + CHUNK], paired, NN)

    def stage_v(start, along):
        if plan.ready:
            part = slice(start, start + CHUNK)
            return near_ref[part], (cube_ref[part] * along).astype(jnp.bfloat16)
        inverse = reciprocal(start, spos)
        cubed = ((inverse * inverse) * (inverse * along)).astype(jnp.bfloat16)
        return inverse.astype(jnp.bfloat16), cubed

    def stage_m(start, kernel, cubed):
        part = slice(start, start + CHUNK)
        ahead = product(kernel, srows[:, :full], NN)
        moments = product(cubed, smom_rows, NN)
        back = None if plan.ready else product(rboth[:, part], kernel, NN)
        backm = product(rmom[:, part], cubed, NN)
        both = rows[part].astype(jnp.float32)
        turn = jnp.sum((both[:, :full] + both[:, full:]) * ahead, axis=1, keepdims=True)
        row_ref[:, part] = jnp.where(lane == 4, turn, moments).T[:8]
        return back, backm

    along = stage_l(0)
    pair = stage_v(0, along)
    for k, start in enumerate(starts):
        if k + 1 < len(starts):
            along = stage_l(starts[k + 1])
        back, backm = stage_m(start, *pair)
        if k + 1 < len(starts):
            pair = stage_v(starts[k + 1], along)
        if k == 0:
            backm_ref[...] = backm
        else:
            backm_ref[...] += backm
        if plan.ready:
            continue
        if k == 0:
            back_ref[...] = back
        else:
            back_ref[...] += back
    if plan.emits:
        rboth_out[...], rows_out[...] = receiving(turns[2])
        points = next_ref[...].astype(jnp.float32)
        for start in starts:
            part = slice(start, start + CHUNK)
            inverse = reciprocal(start, points)
            near_out[part] = inverse.astype(jnp.bfloat16)
            cube_out[part] = inverse * inverse * inverse
    behind = back_ref[: full] + jnp.concatenate(
        [back_ref[full:], jnp.zeros((2 * cols, count), jnp.float32)], axis=0
    )

    def quarter(value, k):
        return value[k * cols : (k + 1) * cols]

    col_turn = wave * jnp.sum(
        quarter(behind, 0) * quarter(send, 3)
        - quarter(behind, 1) * quarter(send, 2)
        + quarter(behind, 2) * quarter(send, 1)
        - quarter(behind, 3) * quarter(send, 0),
        axis=0,
        keepdims=True,
    )
    rm = row_ref[...]
    sm = backm_ref[...]
    row = jnp.concatenate(
        [
            wave * rm[4:5] - ((rpos[0:1] + CHORD_SHIFT) * rm[0:1] - rm[1:2]),
            rm[2:3] - rpos[1:2] * rm[0:1],
            rm[3:4] - rpos[2:3] * rm[0:1],
        ],
        axis=0,
    ) * plan.grad_scale
    col = jnp.concatenate(
        [
            (sm[1:2] + CHORD_SHIFT * sm[0:1] - spos[0:1] * sm[0:1]) - col_turn,
            sm[2:3] - spos[1:2] * sm[0:1],
            sm[3:4] - spos[2:3] * sm[0:1],
        ],
        axis=0,
    ) * plan.grad_scale
    bhigh, blow = halves(behind[: 2 * cols])
    gram = product(jnp.concatenate([bhigh, blow], axis=0), srows, NN)
    gram = (
        gram[: 2 * cols, 2 * cols : full]
        + gram[2 * cols :, 2 * cols : full]
        + gram[: 2 * cols, full : full + 2 * cols]
    )
    force_real = (gram[:cols, :cols] + gram[cols:, cols:]) * plan.force_scale
    force_imag = (gram[:cols, cols:] - gram[cols:, :cols]) * plan.force_scale
    if plan.role == "own":
        grads[0][...] = row + col
        force_ref[0] = force_real
        force_ref[1] = force_imag
    else:
        grads[0][...] = held[0][...] + row
        if plan.last:
            force_real = lanes_from(held[1][0] + force_real)
            force_imag = lanes_from(held[1][1] + force_imag)
            grads[1][...] = jnp.concatenate([col, force_real, force_imag], axis=0)
        else:
            grads[1][...] = col
            force_ref[0] = held[1][0] + force_real
            force_ref[1] = held[1][1] + force_imag


def lanes_from(square):
    side = square.shape[0]
    wide = jnp.concatenate([square[at : at + 8] for at in range(0, side, 8)], axis=1)
    return jnp.concatenate([wide[c : c + 1] for c in range(8)], axis=1)


class Plan:
    def __init__(self, role, last, emits, ready, grad_scale, force_scale):
        self.role = role
        self.last = last
        self.emits = emits
        self.ready = ready
        self.grad_scale = grad_scale
        self.force_scale = force_scale
        self.held = 0 if role == "own" else 2
        self.grads = 1 if role == "own" else 2


def tile_terms(offset, plan, lead, recv, *operands):
    count, width = recv[1].shape
    cols = width // 4
    vmem = pl.BlockSpec(memory_space=pltpu.VMEM)
    grad = jax.ShapeDtypeStruct((3, count), jnp.float32)
    force = jax.ShapeDtypeStruct((2, cols, cols), jnp.float32)
    source = vmem
    extra = []
    outs = (grad,) * plan.grads + (force,)
    if plan.last:
        outs = (grad, jax.ShapeDtypeStruct((5, count), jnp.float32))
    if plan.role == "own":
        source = pl.BlockSpec(memory_space=pltpu.HBM)
        extra = [pltpu.SMEM(part.shape, part.dtype) for part in lead]
        extra.append(pltpu.SemaphoreType.DMA((4,)))
        outs += (pltpu.VMEM((8, width), jnp.float32),)
        outs += tuple(pltpu.VMEM(part.shape, part.dtype) for part in recv)
    if plan.emits:
        outs += (
            pltpu.VMEM((count, count), jnp.bfloat16),
            pltpu.VMEM((count, count), jnp.float32),
            pltpu.VMEM((count, 2 * width), jnp.bfloat16),
            pltpu.VMEM((width + 2 * cols, count), jnp.bfloat16),
        )
    return pl.pallas_call(
        functools.partial(tile_kernel, offset, plan),
        out_shape=outs,
        in_specs=[source] * (len(lead) + 2) + [vmem] * len(operands),
        out_specs=(vmem,) * len(outs),
        scratch_shapes=[
            pltpu.VMEM((width + 2 * cols, count), jnp.float32),
            pltpu.VMEM((16, count), jnp.float32),
            pltpu.VMEM((8, count), jnp.float32),
        ]
        + extra,
        name="tile_%d" % offset,
        compiler_params=pltpu.CompilerParams(vmem_limit_bytes=40 << 20),
        cost_estimate=pl.CostEstimate(
            flops=2 * count * count * width * 6,
            transcendentals=count * count,
            bytes_accessed=4 * count * width,
        ),
    )(*lead, *recv, *operands)


def local(geometry, modes, reduced_freq, freq_index):
    row_count = geometry.shape[1]
    own = (geometry, modes[0])
    columns = modes.shape[2] // 4
    steps = freq_index.shape[1]
    blocks = lax.axis_size("blk")
    freqs = lax.axis_size("freq")
    grad_scale = 1.0 / math.sqrt(columns * steps * row_count * freqs)
    force_scale = 1.0 / math.sqrt(row_count * row_count * blocks * steps)

    def terms(offset, lead, recv, *operands):
        role = "sent" if offset else "own"
        plan = Plan(role, offset == steps - 1, 0 < offset < steps - 1, offset > 1, grad_scale, force_scale)
        return tile_terms(offset, plan, lead, recv, *operands)

    block = passed_along(own[1], "blk", 1)
    points = [passed_along(own[0], "blk", offset) for offset in range(1, steps)]
    placed = [
        pltpu.with_memory_space_constraint(part, pltpu.HBM)
        for part in (reduced_freq, freq_index, *own)
    ]
    mine, force, waves, *kept = terms(0, placed[:2], placed[2:])
    block, points, mine = lax.optimization_barrier((block, points, mine))
    returned = []
    prepared = []
    for offset in range(1, steps):
        current = block
        extra = prepared
        if offset + 1 < steps:
            block = passed_along(block, "blk", 1)
            extra = [points[offset]] + extra
        mine, back, *prepared = terms(
            offset, [waves], kept, points[offset - 1], current, *extra, mine, force
        )
        returned.append(passed_along(back, "blk", -offset))
        force = prepared.pop(0) if prepared else back[3:]
    total = mine
    for back in returned:
        total = total + back[:3]
    if blocks == 4 and steps == 3:
        pair = force + returned[-1][3:]
        force_total = pair + exchanged(pair, "blk", 1)
    else:
        force_total = lax.psum(force, "blk")
    place = lax.axis_index("freq")
    flip = freqs // 2
    while flip:
        half = total.shape[1] // 2
        side = (place // flip) % 2
        kept = lax.dynamic_slice_in_dim(total, side * half, half, axis=1)
        sent = lax.dynamic_slice_in_dim(total, (1 - side) * half, half, axis=1)
        total = kept + exchanged(sent, "freq", flip)
        flip //= 2
    force_total = force_total.reshape(2, 8, columns // 8, columns).transpose(0, 2, 1, 3)
    return (total, force_total.reshape(1, 2, columns, columns))


def solution(mesh):
    return jax.shard_map(
        local,
        mesh=mesh,
        in_specs=(
            P(None, ("case", "blk")),
            P("freq", ("case", "blk"), None),
            P(),
            P(("case", "freq"), None),
        ),
        out_specs=(P(None, ("case", "blk", "freq")), P(("case", "freq"), None, None, None)),
        check_vma=False,
    )
```

```python
import functools
import math

import jax
import jax.numpy as jnp
from jax import lax
from jax.experimental import pallas as pl
from jax.experimental.pallas import tpu as pltpu
from jax.sharding import PartitionSpec as P

CHORD_SHIFT = 0.5
CORE_SQUARE = 0.25
CHUNK = 512

NN = (((1,), (0,)), ((), ()))
NT = (((1,), (1,)), ((), ()))


def passed_along(value, axis, steps):
    count = lax.axis_size(axis)
    pairs = [(source, (source + steps) % count) for source in range(count)]
    return lax.ppermute(value, axis, pairs)


def exchanged(value, axis, flip):
    pairs = [(source, source ^ flip) for source in range(lax.axis_size(axis))]
    return lax.ppermute(value, axis, pairs)


def product(left, right, dims, precision=None):
    return lax.dot_general(
        left, right, dims, preferred_element_type=jnp.float32, precision=precision
    )


def cosine_of(angle):
    turns = jnp.floor(angle * (0.5 / math.pi) + 0.5)
    half = 0.5 * ((angle - turns * 6.28125) - turns * (2.0 * math.pi - 6.28125))
    square = half * half
    value = 1.0 / math.factorial(12)
    for order in (10, 8, 6, 4, 2, 0):
        sign = -1.0 if order % 4 == 2 else 1.0
        value = value * square + sign / math.factorial(order)
    return 2.0 * value * value - 1.0


def turned_modes(flat, cosine, sine):
    cols = flat.shape[0] // 4
    real = [flat[:cols], flat[2 * cols : 3 * cols]]
    imag = [flat[cols : 2 * cols], flat[3 * cols :]]
    parts = []
    for re, im in zip(real, imag):
        parts += [re * cosine - im * sine, re * sine + im * cosine]
    return jnp.concatenate(parts, axis=0)


def crosswise(value):
    cols = value.shape[0] // 4
    p, q, r, s = (value[k * cols : (k + 1) * cols] for k in range(4))
    return jnp.concatenate([-s, r, -q, p], axis=0)


def halves(value):
    high = value.astype(jnp.bfloat16)
    low = (value - high.astype(jnp.float32)).astype(jnp.bfloat16)
    return high, low


def moment_rows(pos):
    count = pos.shape[1]
    return jnp.concatenate(
        [jnp.ones((1, count), jnp.float32), pos, jnp.zeros((12, count), jnp.float32)], axis=0
    ).astype(jnp.bfloat16)


def moment_columns(pos, width):
    rows = moment_rows(pos).astype(jnp.float32)
    still = jnp.zeros((width - rows.shape[0], pos.shape[1]), jnp.float32)
    return jnp.concatenate([rows, still], axis=0).T.astype(jnp.bfloat16)


def tile_kernel(offset, plan, *refs):
    refs = list(refs)

    def taken(number):
        return [refs.pop(0) for _ in range(number)]

    if plan.role == "own":
        table_ref, index_ref, rgeom_ref, rmodes_ref = taken(4)
    else:
        waves_ref, rgeom_ref, rmodes_ref, sgeom_ref, smodes_ref = taken(5)
    if plan.emits:
        (next_ref,) = taken(1)
    if plan.ready:
        near_ref, cube_ref, rows_ref, behind_ref, smom_ref = taken(5)
    held = taken(plan.held)
    grads = taken(plan.grads)
    if not plan.last:
        (force_ref,) = taken(1)
    if plan.role == "own":
        waves_out, geom_out, modes_out = taken(3)
    if plan.emits:
        near_out, cube_out, rows_out, behind_out, smom_out = taken(5)
    back_ref, backm_ref, row_ref = taken(3)
    if plan.ready:
        back_ref = behind_ref
    if plan.role == "own":
        table_buf, index_buf, sems = taken(3)
        copies = [
            pltpu.make_async_copy(rgeom_ref, geom_out, sems.at[0]),
            pltpu.make_async_copy(rmodes_ref, modes_out, sems.at[1]),
            pltpu.make_async_copy(table_ref, table_buf, sems.at[2]),
            pltpu.make_async_copy(index_ref, index_buf, sems.at[3]),
        ]
        for copy in copies:
            copy.start()
        for copy in copies:
            copy.wait()
        rgeom_ref, rmodes_ref = geom_out, modes_out
        wave = table_buf[index_buf[0, offset]]
        for step in range(index_buf.shape[1]):
            value = table_buf[index_buf[0, step]]
            waves_out[step : step + 1] = jnp.full((1, waves_out.shape[1]), value, jnp.float32)
    else:
        wave = waves_ref[offset : offset + 1, 0:1]
    count, full = rmodes_ref.shape
    cols = full // 4
    starts = list(range(0, count, CHUNK))
    rpos = rgeom_ref[...].astype(jnp.float32)
    place = jnp.concatenate([rpos, jnp.zeros((5, count), jnp.float32)], axis=0).T
    if not plan.ready:
        rflat = rmodes_ref[...].astype(jnp.float32).T
    if plan.role == "own":
        spos, sflat = rpos, rflat
    else:
        spos = sgeom_ref[...].astype(jnp.float32)
        sflat = smodes_ref[...].astype(jnp.float32).T
    angles = [wave * spos[0:1]]
    if not plan.ready:
        angles.append(wave * (rpos[0:1] + CHORD_SHIFT))
    if plan.emits:
        angles.append(waves_ref[offset + 1 : offset + 2, 0:1] * (rpos[0:1] + CHORD_SHIFT))
    quarter_turn = 0.5 * math.pi
    circle = cosine_of(
        jnp.concatenate(angles + [angle - quarter_turn for angle in angles], axis=0)
    )
    turns = [(circle[k : k + 1], circle[len(angles) + k :][:1]) for k in range(len(angles))]

    def receiving(turn):
        high, low = halves(turned_modes(rflat, *turn))
        both = jnp.concatenate([high, low[: 2 * cols]], axis=0)
        return both, jnp.concatenate([crosswise(high), crosswise(low)], axis=0).T

    def reciprocal(start, points):
        part = slice(start, start + CHUNK)
        dx = (place[part, 0:1] + CHORD_SHIFT) - points[0:1]
        dy = place[part, 1:2] - points[1:2]
        dz = place[part, 2:3] - points[2:3]
        return lax.rsqrt(dx * dx + dy * dy + (dz * dz + CORE_SQUARE))

    send = turned_modes(sflat, *turns[0])
    shigh, slow = halves(send)
    if plan.ready:
        rows = rows_ref[...]
    else:
        rboth, rows = receiving(turns[1])
    cross = crosswise(jnp.concatenate([shigh[2 * cols :], shigh[: 2 * cols]], axis=0))
    paired = jnp.concatenate([cross, cross], axis=0)
    srows = jnp.concatenate([shigh, slow[2 * cols :], slow[2 * cols :]], axis=0).T
    rmom = moment_rows(rpos)
    smom_rows = smom_ref[...] if plan.ready else moment_columns(spos, full)
    lane = lax.broadcasted_iota(jnp.int32, (CHUNK, full), 1)

    def stage_l(start):
        return product(rows[start : start + CHUNK], paired, NN)

    def stage_v(start, along):
        if plan.ready:
            part = slice(start, start + CHUNK)
            return near_ref[part], (cube_ref[part] * along).astype(jnp.bfloat16)
        inverse = reciprocal(start, spos)
        cubed = ((inverse * inverse) * (inverse * along)).astype(jnp.bfloat16)
        return inverse.astype(jnp.bfloat16), cubed

    def stage_m(start, kernel, cubed):
        part = slice(start, start + CHUNK)
        ahead = product(kernel, srows[:, :full], NN)
        moments = product(cubed, smom_rows, NN)
        back = None if plan.ready else product(rboth[:, part], kernel, NN)
        backm = product(rmom[:, part], cubed, NN)
        both = rows[part].astype(jnp.float32)
        turn = jnp.sum((both[:, :full] + both[:, full:]) * ahead, axis=1, keepdims=True)
        row_ref[:, part] = jnp.where(lane == 4, turn, moments).T[:8]
        return back, backm

    along = stage_l(0)
    pair = stage_v(0, along)
    for k, start in enumerate(starts):
        if k + 1 < len(starts):
            along = stage_l(starts[k + 1])
        back, backm = stage_m(start, *pair)
        if k + 1 < len(starts):
            pair = stage_v(starts[k + 1], along)
        if k == 0:
            backm_ref[...] = backm
        else:
            backm_ref[...] += backm
        if plan.ready:
            continue
        if k == 0:
            back_ref[...] = back
        else:
            back_ref[...] += back
    if plan.emits:
        rboth, rows_out[...] = receiving(turns[2])
        points = next_ref[...].astype(jnp.float32)
        for start in starts:
            part = slice(start, start + CHUNK)
            inverse = reciprocal(start, points)
            near_out[part] = inverse.astype(jnp.bfloat16)
            cube_out[part] = inverse * inverse * inverse
        behind_out[...] = product(rboth, near_out[...], NN)
        smom_out[...] = moment_columns(points, full)
    behind = back_ref[: full] + jnp.concatenate(
        [back_ref[full:], jnp.zeros((2 * cols, count), jnp.float32)], axis=0
    )

    def quarter(value, k):
        return value[k * cols : (k + 1) * cols]

    col_turn = wave * jnp.sum(
        quarter(behind, 0) * quarter(send, 3)
        - quarter(behind, 1) * quarter(send, 2)
        + quarter(behind, 2) * quarter(send, 1)
        - quarter(behind, 3) * quarter(send, 0),
        axis=0,
        keepdims=True,
    )
    rm = row_ref[...]
    sm = backm_ref[...]
    row = jnp.concatenate(
        [
            wave * rm[4:5] - ((rpos[0:1] + CHORD_SHIFT) * rm[0:1] - rm[1:2]),
            rm[2:3] - rpos[1:2] * rm[0:1],
            rm[3:4] - rpos[2:3] * rm[0:1],
        ],
        axis=0,
    ) * plan.grad_scale
    col = jnp.concatenate(
        [
            (sm[1:2] + CHORD_SHIFT * sm[0:1] - spos[0:1] * sm[0:1]) - col_turn,
            sm[2:3] - spos[1:2] * sm[0:1],
            sm[3:4] - spos[2:3] * sm[0:1],
        ],
        axis=0,
    ) * plan.grad_scale
    bhigh, blow = halves(behind[: 2 * cols])
    gram = product(jnp.concatenate([bhigh, blow], axis=0), srows, NN)
    gram = (
        gram[: 2 * cols, 2 * cols : full]
        + gram[2 * cols :, 2 * cols : full]
        + gram[: 2 * cols, full : full + 2 * cols]
    )
    force_real = (gram[:cols, :cols] + gram[cols:, cols:]) * plan.force_scale
    force_imag = (gram[:cols, cols:] - gram[cols:, :cols]) * plan.force_scale
    if plan.role == "own":
        grads[0][...] = row + col
        force_ref[0] = force_real
        force_ref[1] = force_imag
    else:
        grads[0][...] = held[0][...] + row
        if plan.last:
            force_real = lanes_from(held[1][0] + force_real)
            force_imag = lanes_from(held[1][1] + force_imag)
            grads[1][...] = jnp.concatenate([col, force_real, force_imag], axis=0)
        else:
            grads[1][...] = col
            force_ref[0] = held[1][0] + force_real
            force_ref[1] = held[1][1] + force_imag


def lanes_from(square):
    side = square.shape[0]
    wide = jnp.concatenate([square[at : at + 8] for at in range(0, side, 8)], axis=1)
    return jnp.concatenate([wide[c : c + 1] for c in range(8)], axis=1)


class Plan:
    def __init__(self, role, last, emits, ready, grad_scale, force_scale):
        self.role = role
        self.last = last
        self.emits = emits
        self.ready = ready
        self.grad_scale = grad_scale
        self.force_scale = force_scale
        self.held = 0 if role == "own" else 2
        self.grads = 1 if role == "own" else 2


def tile_terms(offset, plan, lead, recv, *operands):
    count, width = recv[1].shape
    cols = width // 4
    vmem = pl.BlockSpec(memory_space=pltpu.VMEM)
    grad = jax.ShapeDtypeStruct((3, count), jnp.float32)
    force = jax.ShapeDtypeStruct((2, cols, cols), jnp.float32)
    source = vmem
    extra = []
    outs = (grad,) * plan.grads + (force,)
    if plan.last:
        outs = (grad, jax.ShapeDtypeStruct((5, count), jnp.float32))
    if plan.role == "own":
        source = pl.BlockSpec(memory_space=pltpu.HBM)
        extra = [pltpu.SMEM(part.shape, part.dtype) for part in lead]
        extra.append(pltpu.SemaphoreType.DMA((4,)))
        outs += (pltpu.VMEM((8, width), jnp.float32),)
        outs += tuple(pltpu.VMEM(part.shape, part.dtype) for part in recv)
    if plan.emits:
        outs += (
            pltpu.VMEM((count, count), jnp.bfloat16),
            pltpu.VMEM((count, count), jnp.float32),
            pltpu.VMEM((count, 2 * width), jnp.bfloat16),
            pltpu.VMEM((width + 2 * cols, count), jnp.float32),
            pltpu.VMEM((count, width), jnp.bfloat16),
        )
    return pl.pallas_call(
        functools.partial(tile_kernel, offset, plan),
        out_shape=outs,
        in_specs=[source] * (len(lead) + 2) + [vmem] * len(operands),
        out_specs=(vmem,) * len(outs),
        scratch_shapes=[
            pltpu.VMEM((width + 2 * cols, count), jnp.float32),
            pltpu.VMEM((16, count), jnp.float32),
            pltpu.VMEM((8, count), jnp.float32),
        ]
        + extra,
        name="tile_%d" % offset,
        compiler_params=pltpu.CompilerParams(vmem_limit_bytes=40 << 20),
        cost_estimate=pl.CostEstimate(
            flops=2 * count * count * width * 6,
            transcendentals=count * count,
            bytes_accessed=4 * count * width,
        ),
    )(*lead, *recv, *operands)


def local(geometry, modes, reduced_freq, freq_index):
    row_count = geometry.shape[1]
    own = (geometry, modes[0])
    columns = modes.shape[2] // 4
    steps = freq_index.shape[1]
    blocks = lax.axis_size("blk")
    freqs = lax.axis_size("freq")
    grad_scale = 1.0 / math.sqrt(columns * steps * row_count * freqs)
    force_scale = 1.0 / math.sqrt(row_count * row_count * blocks * steps)

    def terms(offset, lead, recv, *operands):
        role = "sent" if offset else "own"
        plan = Plan(role, offset == steps - 1, 0 < offset < steps - 1, offset > 1, grad_scale, force_scale)
        return tile_terms(offset, plan, lead, recv, *operands)

    block = passed_along(own[1], "blk", 1)
    points = [passed_along(own[0], "blk", offset) for offset in range(1, steps)]
    placed = [
        pltpu.with_memory_space_constraint(part, pltpu.HBM)
        for part in (reduced_freq, freq_index, *own)
    ]
    mine, force, waves, *kept = terms(0, placed[:2], placed[2:])
    block, points, mine = lax.optimization_barrier((block, points, mine))
    returned = []
    prepared = []
    for offset in range(1, steps):
        current = block
        extra = prepared
        if offset + 1 < steps:
            block = passed_along(block, "blk", 1)
            extra = [points[offset]] + extra
        mine, back, *prepared = terms(
            offset, [waves], kept, points[offset - 1], current, *extra, mine, force
        )
        returned.append(passed_along(back, "blk", -offset))
        force = prepared.pop(0) if prepared else back[3:]
    total = mine
    for back in returned:
        total = total + back[:3]
    if blocks == 4 and steps == 3:
        pair = force + returned[-1][3:]
        force_total = pair + exchanged(pair, "blk", 1)
    else:
        force_total = lax.psum(force, "blk")
    place = lax.axis_index("freq")
    flip = freqs // 2
    while flip:
        half = total.shape[1] // 2
        side = (place // flip) % 2
        kept = lax.dynamic_slice_in_dim(total, side * half, half, axis=1)
        sent = lax.dynamic_slice_in_dim(total, (1 - side) * half, half, axis=1)
        total = kept + exchanged(sent, "freq", flip)
        flip //= 2
    force_total = force_total.reshape(2, 8, columns // 8, columns).transpose(0, 2, 1, 3)
    return (total, force_total.reshape(1, 2, columns, columns))


def solution(mesh):
    return jax.shard_map(
        local,
        mesh=mesh,
        in_specs=(
            P(None, ("case", "blk")),
            P("freq", ("case", "blk"), None),
            P(),
            P(("case", "freq"), None),
        ),
        out_specs=(P(None, ("case", "blk", "freq")), P(("case", "freq"), None, None, None)),
        check_vma=False,
    )
```

```python
import functools
import math

import jax
import jax.numpy as jnp
from jax import lax
from jax.experimental import pallas as pl
from jax.experimental.pallas import tpu as pltpu
from jax.sharding import PartitionSpec as P

CHORD_SHIFT = 0.5
CORE_SQUARE = 0.25
CHUNK = 512

NN = (((1,), (0,)), ((), ()))
NT = (((1,), (1,)), ((), ()))


def passed_along(value, axis, steps):
    count = lax.axis_size(axis)
    pairs = [(source, (source + steps) % count) for source in range(count)]
    return lax.ppermute(value, axis, pairs)


def exchanged(value, axis, flip):
    pairs = [(source, source ^ flip) for source in range(lax.axis_size(axis))]
    return lax.ppermute(value, axis, pairs)


def product(left, right, dims, precision=None):
    return lax.dot_general(
        left, right, dims, preferred_element_type=jnp.float32, precision=precision
    )


def cosine_of(angle):
    turns = jnp.floor(angle * (0.5 / math.pi) + 0.5)
    half = 0.5 * ((angle - turns * 6.28125) - turns * (2.0 * math.pi - 6.28125))
    square = half * half
    value = 1.0 / math.factorial(12)
    for order in (10, 8, 6, 4, 2, 0):
        sign = -1.0 if order % 4 == 2 else 1.0
        value = value * square + sign / math.factorial(order)
    return 2.0 * value * value - 1.0


def turned_modes(flat, cosine, sine):
    cols = flat.shape[0] // 4
    real = [flat[:cols], flat[2 * cols : 3 * cols]]
    imag = [flat[cols : 2 * cols], flat[3 * cols :]]
    parts = []
    for re, im in zip(real, imag):
        parts += [re * cosine - im * sine, re * sine + im * cosine]
    return jnp.concatenate(parts, axis=0)


def crosswise(value):
    cols = value.shape[0] // 4
    p, q, r, s = (value[k * cols : (k + 1) * cols] for k in range(4))
    return jnp.concatenate([-s, r, -q, p], axis=0)


def halves(value):
    high = value.astype(jnp.bfloat16)
    low = (value - high.astype(jnp.float32)).astype(jnp.bfloat16)
    return high, low


def moment_rows(pos):
    count = pos.shape[1]
    return jnp.concatenate(
        [jnp.ones((1, count), jnp.float32), pos, jnp.zeros((12, count), jnp.float32)], axis=0
    ).astype(jnp.bfloat16)


def moment_columns(pos, width):
    rows = moment_rows(pos).astype(jnp.float32)
    still = jnp.zeros((width - rows.shape[0], pos.shape[1]), jnp.float32)
    return jnp.concatenate([rows, still], axis=0).T.astype(jnp.bfloat16)


def tile_kernel(offset, plan, *refs):
    refs = list(refs)

    def taken(number):
        return [refs.pop(0) for _ in range(number)]

    if plan.role == "own":
        table_ref, index_ref, rgeom_ref, rmodes_ref = taken(4)
    else:
        waves_ref, rgeom_ref, rmodes_ref, sgeom_ref, smodes_ref = taken(5)
    if plan.emits:
        (next_ref,) = taken(1)
    if plan.ready:
        near_ref, cube_ref, rows_ref, behind_ref, smom_ref = taken(5)
    held = taken(plan.held)
    grads = taken(plan.grads)
    if not plan.last:
        (force_ref,) = taken(1)
    if plan.role == "own":
        waves_out, geom_out, modes_out = taken(3)
    if plan.emits:
        near_out, cube_out, rows_out, behind_out, smom_out = taken(5)
    back_ref, backm_ref, row_ref = taken(3)
    if plan.ready:
        back_ref = behind_ref
    if plan.role == "own":
        table_buf, index_buf, sems = taken(3)
        copies = [
            pltpu.make_async_copy(rgeom_ref, geom_out, sems.at[0]),
            pltpu.make_async_copy(rmodes_ref, modes_out, sems.at[1]),
            pltpu.make_async_copy(table_ref, table_buf, sems.at[2]),
            pltpu.make_async_copy(index_ref, index_buf, sems.at[3]),
        ]
        for copy in copies:
            copy.start()
        for copy in copies:
            copy.wait()
        rgeom_ref, rmodes_ref = geom_out, modes_out
        wave = table_buf[index_buf[0, offset]]
        for step in range(index_buf.shape[1]):
            value = table_buf[index_buf[0, step]]
            waves_out[step : step + 1] = jnp.full((1, waves_out.shape[1]), value, jnp.float32)
    else:
        wave = waves_ref[offset : offset + 1, 0:1]
    count, full = rmodes_ref.shape
    cols = full // 4
    starts = list(range(0, count, CHUNK))
    rpos = rgeom_ref[...].astype(jnp.float32)
    place = jnp.concatenate([rpos, jnp.zeros((5, count), jnp.float32)], axis=0).T
    if not plan.ready:
        rflat = rmodes_ref[...].astype(jnp.float32).T
    if plan.role == "own":
        spos, sflat = rpos, rflat
    else:
        spos = sgeom_ref[...].astype(jnp.float32)
        sflat = smodes_ref[...].astype(jnp.float32).T
    angles = [wave * spos[0:1]]
    if not plan.ready:
        angles.append(wave * (rpos[0:1] + CHORD_SHIFT))
    if plan.emits:
        angles.append(waves_ref[offset + 1 : offset + 2, 0:1] * (rpos[0:1] + CHORD_SHIFT))
    quarter_turn = 0.5 * math.pi
    circle = cosine_of(
        jnp.concatenate(angles + [angle - quarter_turn for angle in angles], axis=0)
    )
    turns = [(circle[k : k + 1], circle[len(angles) + k :][:1]) for k in range(len(angles))]

    def receiving(turn):
        high, low = halves(turned_modes(rflat, *turn))
        both = jnp.concatenate([high, low[: 2 * cols]], axis=0)
        return both, jnp.concatenate([crosswise(high), crosswise(low)], axis=0).T

    def reciprocal(start, points):
        part = slice(start, start + CHUNK)
        dx = (place[part, 0:1] + CHORD_SHIFT) - points[0:1]
        dy = place[part, 1:2] - points[1:2]
        dz = place[part, 2:3] - points[2:3]
        return lax.rsqrt(dx * dx + dy * dy + (dz * dz + CORE_SQUARE))

    send = turned_modes(sflat, *turns[0])
    shigh, slow = halves(send)
    if plan.ready:
        rows = rows_ref[...]
    else:
        rboth, rows = receiving(turns[1])
    cross = crosswise(jnp.concatenate([shigh[2 * cols :], shigh[: 2 * cols]], axis=0))
    paired = jnp.concatenate([cross, cross], axis=0)
    srows = jnp.concatenate([shigh, slow[2 * cols :], slow[2 * cols :]], axis=0).T
    rmom = moment_rows(rpos)
    smom_rows = smom_ref[...] if plan.ready else moment_columns(spos, full)
    lane = lax.broadcasted_iota(jnp.int32, (CHUNK, full), 1)

    def stage_l(start):
        return product(rows[start : start + CHUNK], paired, NN)

    def stage_v(start, along):
        if plan.ready:
            part = slice(start, start + CHUNK)
            return near_ref[part], (cube_ref[part] * along).astype(jnp.bfloat16)
        inverse = reciprocal(start, spos)
        cubed = ((inverse * inverse) * (inverse * along)).astype(jnp.bfloat16)
        return inverse.astype(jnp.bfloat16), cubed

    def stage_m(start, kernel, cubed):
        part = slice(start, start + CHUNK)
        ahead = product(kernel, srows[:, :full], NN)
        moments = product(cubed, smom_rows, NN)
        back = None if plan.ready else product(rboth[:, part], kernel, NN)
        backm = product(rmom[:, part], cubed, NN)
        both = rows[part].astype(jnp.float32)
        turn = jnp.sum((both[:, :full] + both[:, full:]) * ahead, axis=1, keepdims=True)
        row_ref[:, part] = jnp.where(lane == 4, turn, moments).T[:8]
        return back, backm

    along = stage_l(0)
    pair = stage_v(0, along)
    for k, start in enumerate(starts):
        if k + 1 < len(starts):
            along = stage_l(starts[k + 1])
        back, backm = stage_m(start, *pair)
        if k + 1 < len(starts):
            pair = stage_v(starts[k + 1], along)
        if k == 0:
            backm_ref[...] = backm
        else:
            backm_ref[...] += backm
        if plan.ready:
            continue
        if k == 0:
            back_ref[...] = back
        else:
            back_ref[...] += back
    if plan.emits:
        rboth, rows_out[...] = receiving(turns[2])
        points = next_ref[...].astype(jnp.float32)
        for start in starts:
            part = slice(start, start + CHUNK)
            inverse = reciprocal(start, points)
            near_out[part] = inverse.astype(jnp.bfloat16)
            cube_out[part] = inverse * inverse * inverse
        behind_out[...] = product(rboth, near_out[...], NN)
        smom_out[...] = moment_columns(points, full)
    behind = back_ref[: full] + jnp.concatenate(
        [back_ref[full:], jnp.zeros((2 * cols, count), jnp.float32)], axis=0
    )

    def quarter(value, k):
        return value[k * cols : (k + 1) * cols]

    col_turn = wave * jnp.sum(
        quarter(behind, 0) * quarter(send, 3)
        - quarter(behind, 1) * quarter(send, 2)
        + quarter(behind, 2) * quarter(send, 1)
        - quarter(behind, 3) * quarter(send, 0),
        axis=0,
        keepdims=True,
    )
    rm = row_ref[...]
    sm = backm_ref[...]
    row = jnp.concatenate(
        [
            wave * rm[4:5] - ((rpos[0:1] + CHORD_SHIFT) * rm[0:1] - rm[1:2]),
            rm[2:3] - rpos[1:2] * rm[0:1],
            rm[3:4] - rpos[2:3] * rm[0:1],
        ],
        axis=0,
    ) * plan.grad_scale
    col = jnp.concatenate(
        [
            (sm[1:2] + CHORD_SHIFT * sm[0:1] - spos[0:1] * sm[0:1]) - col_turn,
            sm[2:3] - spos[1:2] * sm[0:1],
            sm[3:4] - spos[2:3] * sm[0:1],
        ],
        axis=0,
    ) * plan.grad_scale
    bhigh, blow = halves(behind[: 2 * cols])
    gram = product(jnp.concatenate([bhigh, blow], axis=0), srows, NN)
    gram = (
        gram[: 2 * cols, 2 * cols : full]
        + gram[2 * cols :, 2 * cols : full]
        + gram[: 2 * cols, full : full + 2 * cols]
    )
    force_real = (gram[:cols, :cols] + gram[cols:, cols:]) * plan.force_scale
    force_imag = (gram[:cols, cols:] - gram[cols:, :cols]) * plan.force_scale
    if plan.role == "own":
        grads[0][...] = row + col
        force_ref[0] = force_real
        force_ref[1] = force_imag
    else:
        grads[0][...] = held[0][...] + row
        if plan.last:
            force_real = lanes_from(held[1][0] + force_real)
            force_imag = lanes_from(held[1][1] + force_imag)
            grads[1][...] = jnp.concatenate([col, force_real, force_imag], axis=0)
        else:
            grads[1][...] = col
            force_ref[0] = held[1][0] + force_real
            force_ref[1] = held[1][1] + force_imag


def lanes_from(square):
    side = square.shape[0]
    wide = jnp.concatenate([square[at : at + 8] for at in range(0, side, 8)], axis=1)
    return jnp.concatenate([wide[c : c + 1] for c in range(8)], axis=1)


class Plan:
    def __init__(self, role, last, emits, ready, grad_scale, force_scale):
        self.role = role
        self.last = last
        self.emits = emits
        self.ready = ready
        self.grad_scale = grad_scale
        self.force_scale = force_scale
        self.held = 0 if role == "own" else 2
        self.grads = 1 if role == "own" else 2


def tile_terms(offset, plan, lead, recv, *operands):
    count, width = recv[1].shape
    cols = width // 4
    vmem = pl.BlockSpec(memory_space=pltpu.VMEM)
    grad = jax.ShapeDtypeStruct((3, count), jnp.float32)
    force = jax.ShapeDtypeStruct((2, cols, cols), jnp.float32)
    source = vmem
    extra = []
    outs = (grad,) * plan.grads + (force,)
    if plan.last:
        outs = (grad, jax.ShapeDtypeStruct((5, count), jnp.float32))
    if plan.role == "own":
        source = pl.BlockSpec(memory_space=pltpu.HBM)
        extra = [pltpu.SMEM(part.shape, part.dtype) for part in lead]
        extra.append(pltpu.SemaphoreType.DMA((4,)))
        outs += (pltpu.VMEM((8, width), jnp.float32),)
        outs += tuple(pltpu.VMEM(part.shape, part.dtype) for part in recv)
    if plan.emits:
        outs += (
            pltpu.VMEM((count, count), jnp.bfloat16),
            pltpu.VMEM((count, count), jnp.float32),
            pltpu.VMEM((count, 2 * width), jnp.bfloat16),
            pltpu.VMEM((width + 2 * cols, count), jnp.float32),
            pltpu.VMEM((count, width), jnp.bfloat16),
        )
    return pl.pallas_call(
        functools.partial(tile_kernel, offset, plan),
        out_shape=outs,
        in_specs=[source] * (len(lead) + 2) + [vmem] * len(operands),
        out_specs=(vmem,) * len(outs),
        scratch_shapes=[
            pltpu.VMEM((width + 2 * cols, count), jnp.float32),
            pltpu.VMEM((16, count), jnp.float32),
            pltpu.VMEM((8, count), jnp.float32),
        ]
        + extra,
        name="tile_%d" % offset,
        compiler_params=pltpu.CompilerParams(vmem_limit_bytes=40 << 20),
        cost_estimate=pl.CostEstimate(
            flops=2 * count * count * width * 6,
            transcendentals=count * count,
            bytes_accessed=4 * count * width,
        ),
    )(*lead, *recv, *operands)


def local(geometry, modes, reduced_freq, freq_index):
    row_count = geometry.shape[1]
    own = (geometry, modes[0])
    columns = modes.shape[2] // 4
    steps = freq_index.shape[1]
    blocks = lax.axis_size("blk")
    freqs = lax.axis_size("freq")
    grad_scale = 1.0 / math.sqrt(columns * steps * row_count * freqs)
    force_scale = 1.0 / math.sqrt(row_count * row_count * blocks * steps)

    def terms(offset, lead, recv, *operands):
        role = "sent" if offset else "own"
        plan = Plan(role, offset == steps - 1, 0 < offset < steps - 1, offset > 1, grad_scale, force_scale)
        return tile_terms(offset, plan, lead, recv, *operands)

    block = passed_along(own[1], "blk", 1)
    points = [passed_along(own[0], "blk", offset) for offset in range(1, steps)]
    placed = [
        pltpu.with_memory_space_constraint(part, pltpu.HBM)
        for part in (reduced_freq, freq_index, *own)
    ]
    mine, force, waves, *kept = terms(0, placed[:2], placed[2:])
    block, points, mine = lax.optimization_barrier((block, points, mine))
    returned = []
    prepared = []
    for offset in range(1, steps):
        current = block
        extra = prepared
        if offset + 1 < steps:
            block = passed_along(block, "blk", 1)
            extra = [points[offset]] + extra
        mine, back, *prepared = terms(
            offset, [waves], kept, points[offset - 1], current, *extra, mine, force
        )
        returned.append(passed_along(back, "blk", -offset))
        force = prepared.pop(0) if prepared else back[3:]
    total = mine
    for back in returned:
        total = total + back[:3]
    if blocks == 4 and steps == 3:
        pair = force + returned[-1][3:]
        force_total = pair + exchanged(pair, "blk", 1)
    else:
        force_total = lax.psum(force, "blk")
    place = lax.axis_index("freq")
    share = row_count // freqs
    flip = 1
    while flip < freqs:
        side = (place // flip) % 2
        groups = total.shape[1] // (2 * share)

        def every_other(first):
            parts = [
                lax.dynamic_slice_in_dim(total, (2 * k + first) * share, share, axis=1)
                for k in range(groups)
            ]
            return jnp.concatenate(parts, axis=1)

        total = every_other(side) + exchanged(every_other(1 - side), "freq", flip)
        flip *= 2
    force_total = force_total.reshape(2, 8, columns // 8, columns).transpose(0, 2, 1, 3)
    return (total, force_total.reshape(1, 2, columns, columns))


def solution(mesh):
    return jax.shard_map(
        local,
        mesh=mesh,
        in_specs=(
            P(None, ("case", "blk")),
            P("freq", ("case", "blk"), None),
            P(),
            P(("case", "freq"), None),
        ),
        out_specs=(P(None, ("case", "blk", "freq")), P(("case", "freq"), None, None, None)),
        check_vma=False,
    )
```
